512 devices in a mesh: row: 32 (over z, x), col: 16 (over y, core).
Axes of the slice: x: 4, y: 8, z: 8, core: 2. Of those that a mesh axis runs over, the one named last changes fastest.
Arguments:
- covariance: float32 [2, 4096, 4, 2048], P(None, 'row', None, 'col'), may hold values from -0.05 to 24.05, as said below
Outputs:
- factored: float32 [2, 4096, 4, 2048], P(None, 'row', None, 'col')
The draws below stay inside these ranges and needn't reach their ends.
Inputs may be any that keep to these rules, and one draw needn't show every extreme that they name: covariance holds a symmetric matrix whose leading principal block of order 3 * 128 is positive definite.
All inputs are finite; a program needn't handle non-finite values.
Results may differ from the reference program's by a relative error of at most 0.0002.
Values sent between devices are 32-bit elements; how exact they have to be, the bound alone decides.
No kernel may reach another device: no remote copies, remote signals or barrier semaphores. Data moves between devices by JAX's collectives and lax.ppermute only.
A program may use at most 64 MiB of HBM per device.

```python
import jax
import jax.numpy as jnp
from jax import lax

NB = 128
TR = 2
PANELS = 3
TC = 4
ORDER = 8192
N_ROW = 32
N_COL = 16


def draw_covariance(key, part):
    matrix_order = ORDER
    keys = jax.random.split(key, 4)
    place_x = jax.random.uniform(keys[0], (matrix_order,), jnp.float32)
    place_y = jax.random.uniform(keys[1], (matrix_order,), jnp.float32)
    weights = jax.random.uniform(keys[2], (matrix_order,), jnp.float32, 1.0, 2.0)
    phases = jax.random.uniform(keys[3], (matrix_order,), jnp.float32, -jnp.pi, jnp.pi)
    length_scale = 0.1
    distance = jnp.sqrt((place_x[:, None] - place_x[None, :]) ** 2 + (place_y[:, None] - place_y[None, :]) ** 2)
    kernel = 4.0 * jnp.exp(-distance / length_scale)
    noise = 0.05 * jnp.cos(200.0 * weights[:, None] * weights[None, :] + phases[:, None] + phases[None, :])
    index = jnp.arange(matrix_order, dtype=jnp.int32)
    nugget = jnp.where(index[:, None] == index[None, :], 20.0, 0.0)
    full = kernel + noise + nugget
    return full.astype(jnp.float32).reshape(TR, N_ROW * NB, TC, N_COL * NB)


def setup_inputs(seed: int = 0) -> dict:
    key_list = jax.random.split(jax.random.key(seed), 2)
    return {
        "covariance": draw_covariance(jax.random.fold_in(key_list[1], 71), 0),
    }


def reference(covariance):
    matrix_order = covariance.shape[0] * covariance.shape[1]
    matrix = covariance.reshape(matrix_order, matrix_order)
    for panel_index in range(PANELS):
        first_row = panel_index * NB
        last_row = first_row + NB
        factor = jnp.linalg.cholesky(matrix[first_row:last_row, first_row:last_row])
        below_rows = matrix[last_row:, first_row:last_row]
        solved = jax.scipy.linalg.solve_triangular(factor, below_rows.T, lower=True).T
        trailing = matrix[last_row:, last_row:] - jnp.dot(solved.astype(jnp.float32), solved.T.astype(jnp.float32), precision=lax.Precision.HIGHEST, preferred_element_type=jnp.float32)
        matrix = matrix.at[last_row:, last_row:].set(trailing)
        matrix = matrix.at[first_row:last_row, first_row:last_row].set(factor)
        matrix = matrix.at[last_row:, first_row:last_row].set(solved)
    return jnp.tril(matrix).reshape(covariance.shape)
```

```python
import jax
import jax.numpy as jnp
from jax import lax
from jax.sharding import PartitionSpec as P

PANELS = 3
UPPER = [(i, j) for i in range(PANELS) for j in range(i, PANELS)]


def mm(a, b):
    return jnp.dot(a, b, precision=lax.Precision.HIGHEST, preferred_element_type=jnp.float32)


def gather_leading_rows(matrix, row_count, col_count):
    tile_rows, nb, tile_cols, _ = matrix.shape
    part = nb // row_count
    split = matrix[0].reshape(row_count, part, tile_cols, nb).transpose(0, 2, 1, 3)
    piece = lax.all_to_all(split, "row", 0, 0)[:PANELS]
    everyone = lax.all_gather(piece, "col")
    groups = row_count // col_count
    by_row = everyone.reshape(col_count, PANELS, tile_rows, groups, part, nb)
    by_row = by_row.transpose(3, 0, 1, 2, 4, 5).reshape(row_count, PANELS * tile_rows, part, nb)
    lead = jnp.stack([everyone[j, i, 0] for i, j in UPPER])
    lead = jnp.broadcast_to(lead[None], (row_count,) + lead.shape)
    mine = piece.reshape(1, PANELS * tile_cols, part, nb)
    mine = jnp.broadcast_to(mine, (row_count,) + mine.shape[1:])
    packed = jnp.concatenate([mine, by_row, lead], axis=1)
    count = packed.shape[1]
    packed = packed.reshape(row_count, count * part, nb)
    got = lax.all_to_all(packed, "row", 0, 0)
    tiles = got.reshape(row_count, count, part, nb).transpose(1, 0, 2, 3).reshape(count, nb, nb)
    y_tiles = tiles[: PANELS * tile_cols].reshape(PANELS, tile_cols, nb, nb)
    x_tiles = tiles[PANELS * tile_cols : PANELS * (tile_cols + tile_rows)].reshape(PANELS, tile_rows, nb, nb)
    lead_tiles = tiles[PANELS * (tile_cols + tile_rows) :]
    return lead_tiles, x_tiles, y_tiles


def per_device(matrix):
    tile_rows, nb, tile_cols, _ = matrix.shape
    row_count = lax.axis_size("row")
    col_count = lax.axis_size("col")
    my_row = lax.axis_index("row")
    my_col = lax.axis_index("col")
    lead_tiles, x_tiles, y_tiles = gather_leading_rows(matrix, row_count, col_count)
    lead = dict(zip(UPPER, [lead_tiles[n] for n in range(len(UPPER))]))
    rest = [
        jnp.concatenate([x_tiles[i, t] for t in range(tile_rows)] + [y_tiles[i, s] for s in range(tile_cols)], axis=1)
        for i in range(PANELS)
    ]
    eye = jnp.eye(nb, dtype=jnp.float32)
    solved = []
    for k in range(PANELS):
        factor = jnp.linalg.cholesky(lead[k, k])
        inverse = jax.scipy.linalg.solve_triangular(factor, eye, lower=True)
        wide = jnp.concatenate([lead[k, j] for j in range(k + 1, PANELS)] + [rest[k]], axis=1)
        wide = mm(inverse, wide)
        skip = (PANELS - 1 - k) * nb
        solved.append(wide[:, skip:])
        for i in range(k + 1, PANELS):
            left = wide[:, (i - k - 1) * nb : (i - k) * nb].T
            change = mm(left, wide[:, (i - k - 1) * nb :])
            for j in range(i, PANELS):
                lead[i, j] = lead[i, j] - change[:, (j - i) * nb : (j - i + 1) * nb]
            rest[i] = rest[i] - change[:, (PANELS - i) * nb :]
    upper = jnp.concatenate(solved, axis=0)
    rows_t = upper[:, : tile_rows * nb]
    cols = upper[:, tile_rows * nb :]
    product = lax.dot_general(rows_t, cols, (((0,), (0,)), ((), ())), precision=lax.Precision.HIGHEST)
    result = matrix - product.reshape(tile_rows, nb, tile_cols, nb)
    panel = jnp.stack([s[:, : tile_rows * nb] for s in solved])
    panel = lax.dynamic_index_in_dim(panel, jnp.minimum(my_col, PANELS - 1), 0, keepdims=False).T
    panel = panel.reshape(tile_rows, nb, nb)
    owner = (jnp.arange(tile_cols) == 0) & (my_col < PANELS)
    result = jnp.where(owner[None, None, :, None], panel[:, :, None, :], result)
    row_blocks = jnp.arange(tile_rows, dtype=jnp.int32) * row_count + my_row
    col_blocks = jnp.arange(tile_cols, dtype=jnp.int32) * col_count + my_col
    within = jnp.arange(nb, dtype=jnp.int32)
    rows_global = row_blocks[:, None] * nb + within[None, :]
    cols_global = col_blocks[:, None] * nb + within[None, :]
    lower_mask = rows_global[:, :, None, None] >= cols_global[None, None, :, :]
    return jnp.where(lower_mask, result, jnp.zeros_like(result))


def solution(mesh):
    placed = (P(None, "row", None, "col"),)
    return jax.shard_map(
        per_device,
        mesh=mesh,
        in_specs=placed,
        out_specs=P(None, "row", None, "col"),
        check_vma=False,
    )
```

```python
import jax
import jax.numpy as jnp
from jax import lax
from jax.experimental import pallas as pl
from jax.experimental.pallas import tpu as pltpu
from jax.sharding import PartitionSpec as P


NB = 128
PANELS = 3
STRIP = 16
NX = 4
NZ = 8
PART = NB // NZ
UPPER = [(i, j) for i in range(PANELS) for j in range(i, PANELS)]
VMEM = pl.BlockSpec(memory_space=pltpu.VMEM)
SMEM = pl.BlockSpec(memory_space=pltpu.SMEM)


def mm(a, b):
    return jnp.dot(a, b, precision=lax.Precision.HIGHEST, preferred_element_type=jnp.float32)


def factor_strip(strip, first):
    n = strip.shape[0]
    rows = lax.broadcasted_iota(jnp.int32, (n, NB), 0)
    cols = [jnp.broadcast_to(strip[:, first + i : first + i + 1], (n, NB)) for i in range(n)]
    parts = [strip[:, q * NB : (q + 1) * NB] for q in range(strip.shape[1] // NB)]
    upper = list(parts)
    pivots = jnp.ones((n, NB), jnp.float32)
    for i in range(n):
        here = rows == i
        pivot = jnp.broadcast_to(cols[i][i : i + 1, :], (n, NB))
        scale = 1.0 / pivot
        pivots = jnp.where(here, pivot, pivots)
        lift = jnp.where(here, 0.0, cols[i] * scale)
        for j in range(i + 1, n):
            cols[j] = cols[j] - lift * jnp.broadcast_to(cols[j][i : i + 1, :], (n, NB))
        upper = [jnp.where(here, p, u) for p, u in zip(parts, upper)]
        parts = [p - lift * jnp.broadcast_to(p[i : i + 1, :], (n, NB)) for p in parts]
    root = lax.rsqrt(pivots)
    inverse = 1.0 / pivots
    upper = jnp.concatenate([u * root for u in upper], axis=1)
    solved = jnp.concatenate([p * inverse for p in parts], axis=1)
    return upper, solved


def factor_kernel(lead_ref, inv_ref, low_ref, work, upper):
    eye = lax.broadcasted_iota(jnp.int32, (NB, NB), 0) == lax.broadcasted_iota(jnp.int32, (NB, NB), 1)
    eye = eye.astype(jnp.float32)
    zero = jnp.zeros((NB, NB), jnp.float32)
    for k in range(PANELS):
        for q, j in zip((0, 2, 3), (k, k + 1, k + 2)):
            tile = lead_ref[:, UPPER.index((k, j)) * PART :, :][:, :PART, :].reshape(NB, NB) if j < PANELS else zero
            work[k, :, q * NB : (q + 1) * NB] = tile
        work[k, :, NB : 2 * NB] = eye

    def panel(k, carry):
        strip = work[k, 0:STRIP, :]
        for b in range(NB // STRIP):
            first = b * STRIP
            rows_u, solved = factor_strip(strip, first)
            upper[first : first + STRIP, :] = rows_u
            rest = NB - first - STRIP
            if rest:
                pieces = [jnp.zeros((first, 4 * NB), jnp.float32)] if first else []
                pieces += [solved, jnp.zeros((rest, 4 * NB), jnp.float32)]
                padded = jnp.concatenate(pieces, axis=0)
                below = work[k, first + STRIP :, :]
                below = below - mm(below[:, :NB], padded)
                strip = below[:STRIP]
                if rest > STRIP:
                    work[k, first + 2 * STRIP :, :] = below[STRIP:]
        inv_ref[k] = upper[:, NB : 2 * NB]

        @pl.when(k < PANELS - 1)
        def _():
            u1 = upper[:, 2 * NB : 3 * NB]
            u2 = upper[:, 3 * NB :]
            l1 = u1.T
            l2 = u2.T
            low_ref[k, 0] = l1
            low_ref[k, 1] = l2
            work[k + 1, :, :NB] -= mm(l1, u1)
            work[k + 1, :, 2 * NB : 3 * NB] -= mm(l1, u2)
            work[k + 2, :, :NB] -= mm(l2, u2)

        return carry

    lax.fori_loop(0, PANELS, panel, 0)


def factor(lead):
    return pl.pallas_call(
        factor_kernel,
        out_shape=(
            jax.ShapeDtypeStruct((PANELS, NB, NB), jnp.float32),
            jax.ShapeDtypeStruct((PANELS - 1, 2, NB, NB), jnp.float32),
        ),
        in_specs=[VMEM],
        out_specs=[VMEM, VMEM],
        scratch_shapes=[
            pltpu.VMEM((PANELS + 1, NB, 4 * NB), jnp.float32),
            pltpu.VMEM((NB, 4 * NB), jnp.float32),
        ],
        name="factor",
    )(lead)


def mm_nt(a, b):
    return lax.dot_general(
        a, b, (((1,), (1,)), ((), ())), precision=lax.Precision.HIGHEST, preferred_element_type=jnp.float32
    )


def pack_kernel(place_ref, own_ref, one_ref, two_ref, three_ref, out_ref, got):
    for d, ref in enumerate((own_ref, one_ref, two_ref, three_ref)):
        got[d] = ref[...]
    my_x = lax.rem(place_ref[0], NX)
    for p, (i, j) in enumerate(UPPER):
        tile = got[lax.rem(my_x + NX - i, NX), j * PART : (j + 1) * PART, :]
        for z in range(NZ):
            out_ref[z, p * PART : (p + 1) * PART, :] = tile


def pack(place, pieces):
    shape = pieces[0].shape
    return pl.pallas_call(
        pack_kernel,
        out_shape=jax.ShapeDtypeStruct((NZ, len(UPPER) * PART, NB), jnp.float32),
        in_specs=[SMEM] + [VMEM] * len(pieces),
        out_specs=VMEM,
        scratch_shapes=[pltpu.VMEM((len(pieces),) + shape, jnp.float32)],
        name="pack",
    )(place, *pieces)


def finish_kernel(place_ref, inv_ref, low_ref, x_ref, y_ref, m_ref, out_ref):
    my_row = place_ref[0]
    my_col = place_ref[1]
    col_count = place_ref[2]
    row_count = NX * NZ
    odd = lax.rem(my_col // 2, 2)
    left = [x_ref[0, odd], x_ref[1, odd], x_ref[0, 1 - odd]]
    rows0 = mm_nt(left[0], inv_ref[0])
    rows1 = mm_nt(left[1] - mm_nt(rows0, low_ref[0, 0]), inv_ref[1])
    rows2 = mm_nt(left[2] - mm_nt(rows0, low_ref[0, 1]) - mm_nt(rows1, low_ref[1, 0]), inv_ref[2])
    right = []
    for i in range(PANELS):
        right.append(jnp.concatenate([y_ref[i, pl.ds(s, NB, stride=4), :] for s in range(4)], axis=1))
    cols0 = mm(inv_ref[0], right[0])
    cols1 = mm(inv_ref[1], right[1] - mm(low_ref[0, 0], cols0))
    cols2 = mm(inv_ref[2], right[2] - mm(low_ref[0, 1], cols0) - mm(low_ref[1, 0], cols1))
    rows = jnp.concatenate([rows0, rows1, rows2], axis=1)
    product = mm(rows, jnp.concatenate([cols0, cols1, cols2], axis=0))
    panel = jnp.where(my_col == 0, rows0, jnp.where(my_col == 1, rows1, rows2))
    u = lax.broadcasted_iota(jnp.int32, (NB, NB), 0)
    v = lax.broadcasted_iota(jnp.int32, (NB, NB), 1)
    for t in range(2):
        for s in range(4):
            value = m_ref[t, pl.ds(s, NB, stride=4), :] - product[t * NB : (t + 1) * NB, s * NB : (s + 1) * NB]
            if s == 0:
                value = jnp.where(my_col < PANELS, panel[t * NB : (t + 1) * NB], value)
            below = (t * row_count + my_row - s * col_count - my_col) * NB
            out_ref[t, pl.ds(s, NB, stride=4), :] = jnp.where(below + u >= v, value, 0.0)


def finish(place, inverse, low, x_part, y_part, matrix):
    return pl.pallas_call(
        finish_kernel,
        out_shape=jax.ShapeDtypeStruct(matrix.shape, jnp.float32),
        in_specs=[SMEM] + [VMEM] * 5,
        out_specs=VMEM,
        name="finish",
    )(place, inverse, low, x_part, y_part, matrix)


def to_all(value, axis, groups):
    count = len(groups[0])
    return lax.all_to_all(jnp.broadcast_to(value[None], (count,) + value.shape), axis, 0, 0, axis_index_groups=groups)


def per_device(covariance):
    tile_rows, nb, tile_cols, _ = covariance.shape
    col_count = lax.axis_size("col")
    my_col = lax.axis_index("col")
    place = jnp.stack([lax.axis_index("row"), my_col, jnp.int32(col_count)])
    matrix = covariance.reshape(tile_rows, nb * tile_cols, nb)
    along_z = [[z * NX + x for z in range(NZ)] for x in range(NX)]
    along_y = [[c for c in range(q, col_count, 2)] for q in range(2)]
    pairs = [[c, c + 1] for c in range(0, col_count, 2)]
    half, quarter = col_count // 2, col_count // 4

    mine = covariance[:, :, 0, :].reshape(tile_rows * nb, nb)
    far = lax.ppermute(mine, "col", [(c, c + half) for c in range(PANELS)])
    mine = jnp.where(my_col >= half, far, mine)
    mid = lax.ppermute(mine, "col", [(c + h, c + h + quarter) for c in range(PANELS) for h in (0, half)])
    mine = jnp.where(my_col % half >= quarter, mid, mine)
    steps = []
    for start in range(0, col_count, quarter):
        steps += [(start, start + 2), (start + 1, start + 3), (start + 2, start)]
    near = lax.ppermute(mine, "col", steps)
    x_part = lax.all_gather(jnp.stack([mine, near]), "col", axis_index_groups=pairs)

    piece = lax.all_to_all(matrix[0].reshape(NZ, PART * tile_cols, nb), "row", 0, 0, axis_index_groups=along_z)[0]
    y_block = to_all(piece, "row", along_z).reshape(nb * tile_cols, nb)
    head = piece.reshape(PART, tile_cols, nb)[:, 0, :]
    own = to_all(head, "col", along_y)[:2]
    both = lax.all_gather(own, "col", axis_index_groups=pairs)
    lead = jnp.concatenate([both[j % 2, j // 2] for j in range(PANELS)], axis=0)
    pieces = [lead]
    for d in range(1, NX):
        hops = [(z * NX + x, z * NX + (x + d) % NX) for z in range(NZ) for x in range(PANELS)]
        pieces.append(lax.ppermute(lead, "row", hops))
    lead = pack(place, pieces)
    lead = lax.all_to_all(lead, "row", 0, 0, axis_index_groups=along_z)
    along_x = [[z * NX + x for x in range(NX)] for z in range(NZ)]
    y_part = to_all(y_block, "row", along_x)
    inverse, low = factor(lead)
    out = finish(place, inverse, low, x_part, y_part, matrix)
    return out.reshape(covariance.shape)


def solution(mesh):
    placed = (P(None, "row", None, "col"),)
    return jax.shard_map(
        per_device,
        mesh=mesh,
        in_specs=placed,
        out_specs=P(None, "row", None, "col"),
        check_vma=False,
    )
```

```python
import jax
import jax.numpy as jnp
from jax import lax
from jax.experimental import pallas as pl
from jax.experimental.pallas import tpu as pltpu
from jax.sharding import PartitionSpec as P


NB = 128
PANELS = 3
STRIP = 16
NX = 4
NZ = 8
PART = NB // NZ
VMEM = pl.BlockSpec(memory_space=pltpu.VMEM)
SMEM = pl.BlockSpec(memory_space=pltpu.SMEM)


def mm(a, b):
    return jnp.dot(a, b, precision=lax.Precision.HIGHEST, preferred_element_type=jnp.float32)


def factor_strip(strip, first):
    n = strip.shape[0]
    rows = lax.broadcasted_iota(jnp.int32, (n, NB), 0)
    cols = [jnp.broadcast_to(strip[:, first + i : first + i + 1], (n, NB)) for i in range(n)]
    parts = [strip[:, q * NB : (q + 1) * NB] for q in range(strip.shape[1] // NB)]
    upper = list(parts)
    pivots = jnp.ones((n, NB), jnp.float32)
    for i in range(n):
        here = rows == i
        pivot = jnp.broadcast_to(cols[i][i : i + 1, :], (n, NB))
        scale = 1.0 / pivot
        pivots = jnp.where(here, pivot, pivots)
        lift = jnp.where(here, 0.0, cols[i] * scale)
        for j in range(i + 1, n):
            cols[j] = cols[j] - lift * jnp.broadcast_to(cols[j][i : i + 1, :], (n, NB))
        upper = [jnp.where(here, p, u) for p, u in zip(parts, upper)]
        parts = [p - lift * jnp.broadcast_to(p[i : i + 1, :], (n, NB)) for p in parts]
    root = lax.rsqrt(pivots)
    inverse = 1.0 / pivots
    upper = jnp.concatenate([u * root for u in upper], axis=1)
    solved = jnp.concatenate([p * inverse for p in parts], axis=1)
    return upper, solved


def factor_kernel(lead_ref, inv_ref, low_ref, work, upper):
    eye = lax.broadcasted_iota(jnp.int32, (NB, NB), 0) == lax.broadcasted_iota(jnp.int32, (NB, NB), 1)
    eye = eye.astype(jnp.float32)
    zero = jnp.zeros((NB, NB), jnp.float32)

    def tile(core, n):
        return lead_ref[core, :, n * PART : (n + 1) * PART, :].reshape(NB, NB)

    rows = ((tile(0, 0), tile(1, 0), tile(0, 1)), (tile(1, 1), tile(1, 2).T, zero), (tile(0, 2), zero, zero))
    for k, tiles in enumerate(rows):
        for q, value in zip((0, 2, 3), tiles):
            work[k, :, q * NB : (q + 1) * NB] = value
        work[k, :, NB : 2 * NB] = eye

    def panel(k, carry):
        strip = work[k, 0:STRIP, :]
        for b in range(NB // STRIP):
            first = b * STRIP
            rows_u, solved = factor_strip(strip, first)
            upper[first : first + STRIP, :] = rows_u
            rest = NB - first - STRIP
            if rest:
                pieces = [jnp.zeros((first, 4 * NB), jnp.float32)] if first else []
                pieces += [solved, jnp.zeros((rest, 4 * NB), jnp.float32)]
                padded = jnp.concatenate(pieces, axis=0)
                below = work[k, first + STRIP :, :]
                below = below - mm(below[:, :NB], padded)
                strip = below[:STRIP]
                if rest > STRIP:
                    work[k, first + 2 * STRIP :, :] = below[STRIP:]
        inv_ref[k] = upper[:, NB : 2 * NB]

        @pl.when(k < PANELS - 1)
        def _():
            u1 = upper[:, 2 * NB : 3 * NB]
            u2 = upper[:, 3 * NB :]
            l1 = u1.T
            l2 = u2.T
            low_ref[k, 0] = l1
            low_ref[k, 1] = l2
            work[k + 1, :, :NB] -= mm(l1, u1)
            work[k + 1, :, 2 * NB : 3 * NB] -= mm(l1, u2)
            work[k + 2, :, :NB] -= mm(l2, u2)

        return carry

    lax.fori_loop(0, PANELS, panel, 0)


def factor(lead):
    return pl.pallas_call(
        factor_kernel,
        out_shape=(
            jax.ShapeDtypeStruct((PANELS, NB, NB), jnp.float32),
            jax.ShapeDtypeStruct((PANELS - 1, 2, NB, NB), jnp.float32),
        ),
        in_specs=[VMEM],
        out_specs=[VMEM, VMEM],
        scratch_shapes=[
            pltpu.VMEM((PANELS + 1, NB, 4 * NB), jnp.float32),
            pltpu.VMEM((NB, 4 * NB), jnp.float32),
        ],
        name="factor",
    )(lead)


def mm_nt(a, b):
    return lax.dot_general(
        a, b, (((1,), (1,)), ((), ())), precision=lax.Precision.HIGHEST, preferred_element_type=jnp.float32
    )


def pack_lead_kernel(got_ref, lead_ref):
    core = lax.rem(lax.axis_index("col"), 2)
    for n, block in enumerate((0, core, 2)):
        at = pl.multiple_of((0 if n == 0 else 1 - core) * PART, PART)
        tile = got_ref[block, pl.ds(at, PART), :]
        for z in range(NZ):
            lead_ref[z, n * PART : (n + 1) * PART, :] = tile


def pack_cols_kernel(got_ref, cols_ref):
    size = got_ref.shape[1] - 2 * PART
    for i in range(PANELS):
        tile = got_ref[i, 2 * PART :, :]
        for z in range(NZ):
            cols_ref[z, i * size : (i + 1) * size, :] = tile


def pack(kernel, got, rows):
    return pl.pallas_call(
        kernel, out_shape=jax.ShapeDtypeStruct((NZ, rows, NB), jnp.float32), in_specs=[VMEM], out_specs=VMEM
    )(got)


def finish_kernel(inv_ref, low_ref, mine_ref, other_ref, y_ref, m_ref, out_ref, x_got):
    my_row = lax.axis_index("row")
    my_col = lax.axis_index("col")
    col_count = lax.axis_size("col")
    row_count = NX * NZ
    core = lax.rem(my_col, 2)
    odd = lax.rem(my_col // 2, 2)
    x_got[core] = mine_ref[...]
    x_got[1 - core] = other_ref[...]
    left = [x_got[0, odd], x_got[1, odd], x_got[0, 1 - odd]]
    rows0 = mm_nt(left[0], inv_ref[0])
    rows1 = mm_nt(left[1] - mm_nt(rows0, low_ref[0, 0]), inv_ref[1])
    rows2 = mm_nt(left[2] - mm_nt(rows0, low_ref[0, 1]) - mm_nt(rows1, low_ref[1, 0]), inv_ref[2])
    right = []
    for i in range(PANELS):
        tiles = []
        for s in range(4):
            at = i * PART * 4 + s
            tiles.append(jnp.concatenate([y_ref[z, pl.ds(at, PART, stride=4), :] for z in range(NZ)], axis=0))
        right.append(jnp.concatenate(tiles, axis=1))
    cols0 = mm(inv_ref[0], right[0])
    cols1 = mm(inv_ref[1], right[1] - mm(low_ref[0, 0], cols0))
    cols2 = mm(inv_ref[2], right[2] - mm(low_ref[0, 1], cols0) - mm(low_ref[1, 0], cols1))
    rows = jnp.concatenate([rows0, rows1, rows2], axis=1)
    product = mm(rows, jnp.concatenate([cols0, cols1, cols2], axis=0))
    panel = jnp.where(my_col == 0, rows0, jnp.where(my_col == 1, rows1, rows2))
    u = lax.broadcasted_iota(jnp.int32, (NB, NB), 0)
    v = lax.broadcasted_iota(jnp.int32, (NB, NB), 1)
    for t in range(2):
        for s in range(4):
            value = m_ref[t, pl.ds(s, NB, stride=4), :] - product[t * NB : (t + 1) * NB, s * NB : (s + 1) * NB]
            if s == 0:
                value = jnp.where(my_col < PANELS, panel[t * NB : (t + 1) * NB], value)
            below = (t * row_count + my_row - s * col_count - my_col) * NB
            out_ref[t, pl.ds(s, NB, stride=4), :] = jnp.where(below + u >= v, value, 0.0)


def finish(inverse, low, mine, other, y_part, matrix):
    return pl.pallas_call(
        finish_kernel,
        out_shape=jax.ShapeDtypeStruct(matrix.shape, jnp.float32),
        in_specs=[VMEM] * 6,
        out_specs=VMEM,
        scratch_shapes=[pltpu.VMEM((2,) + mine.shape, jnp.float32)],
        name="finish",
    )(inverse, low, mine, other, y_part, matrix)


def to_all(value, axis, groups):
    count = len(groups[0])
    return lax.all_to_all(jnp.broadcast_to(value[None], (count,) + value.shape), axis, 0, 0, axis_index_groups=groups)


def per_device(covariance):
    tile_rows, nb, tile_cols, _ = covariance.shape
    col_count = lax.axis_size("col")
    my_col = lax.axis_index("col")
    matrix = covariance.reshape(tile_rows, nb * tile_cols, nb)
    along_z = [[z * NX + x for z in range(NZ)] for x in range(NX)]
    along_x = [[z * NX + x for x in range(NX)] for z in range(NZ)]
    along_y = [[c for c in range(q, col_count, 2)] for q in range(2)]
    pairs = [[c, c + 1] for c in range(0, col_count, 2)]
    half, quarter = col_count // 2, col_count // 4

    mine = covariance[:, :, 0, :].reshape(tile_rows * nb, nb)
    far = lax.ppermute(mine, "col", [(c, c + half) for c in range(PANELS)])
    mine = jnp.where(my_col >= half, far, mine)
    mid = lax.ppermute(mine, "col", [(c + h, c + h + quarter) for c in range(PANELS) for h in (0, half)])
    mine = jnp.where(my_col % half >= quarter, mid, mine)
    steps = []
    for start in range(0, col_count, quarter):
        steps += [(start, start + 2), (start + 1, start + 3), (start + 2, start)]
    near = lax.ppermute(mine, "col", steps)
    panels = jnp.stack([mine, near])
    other = lax.ppermute(panels, "col", [(c, c ^ 1) for c in range(col_count)])

    piece = lax.all_to_all(matrix[0].reshape(NZ, PART * tile_cols, nb), "row", 0, 0, axis_index_groups=along_z)[0]
    head = piece.reshape(PART, tile_cols, nb)[:, 0, :]
    own = to_all(head, "col", along_y)[:2]
    got = to_all(jnp.concatenate([own.reshape(2 * PART, nb), piece], axis=0), "row", along_x)
    lead = pack(pack_lead_kernel, got, PANELS * PART)
    lead = lax.all_to_all(lead, "row", 0, 0, axis_index_groups=along_z)
    lead = lax.all_gather(lead, "col", axis_index_groups=pairs)
    cols = pack(pack_cols_kernel, got, PANELS * PART * tile_cols)
    y_part = lax.all_to_all(cols, "row", 0, 0, axis_index_groups=along_z)
    inverse, low = factor(lead)
    out = finish(inverse, low, panels, other, y_part, matrix)
    return out.reshape(covariance.shape)


def solution(mesh):
    placed = (P(None, "row", None, "col"),)
    return jax.shard_map(
        per_device,
        mesh=mesh,
        in_specs=placed,
        out_specs=P(None, "row", None, "col"),
        check_vma=False,
    )
```

```python
import jax
import jax.numpy as jnp
from jax import lax
from jax.experimental import pallas as pl
from jax.experimental.pallas import tpu as pltpu
from jax.sharding import PartitionSpec as P


NB = 128
PANELS = 3
STRIP = 16
NX = 4
NZ = 8
PART = NB // NZ
VMEM = pl.BlockSpec(memory_space=pltpu.VMEM)
SMEM = pl.BlockSpec(memory_space=pltpu.SMEM)


def mm(a, b):
    return jnp.dot(a, b, precision=lax.Precision.HIGHEST, preferred_element_type=jnp.float32)


def mm3(a, b, contract=(1, 0)):
    a_high, b_high = a.astype(jnp.bfloat16), b.astype(jnp.bfloat16)
    a_low = (a - a_high.astype(jnp.float32)).astype(jnp.bfloat16)
    b_low = (b - b_high.astype(jnp.float32)).astype(jnp.bfloat16)
    dims = (((contract[0],), (contract[1],)), ((), ()))

    def dot(p, q):
        return lax.dot_general(p, q, dims, preferred_element_type=jnp.float32)

    return dot(a_high, b_high) + (dot(a_high, b_low) + dot(a_low, b_high))


def factor_strip(strip, first):
    n = strip.shape[0]
    rows = lax.broadcasted_iota(jnp.int32, (n, NB), 0)
    cols = [jnp.broadcast_to(strip[:, first + i : first + i + 1], (n, NB)) for i in range(n)]
    parts = [strip[:, q * NB : (q + 1) * NB] for q in range(strip.shape[1] // NB)]
    upper = list(parts)
    pivots = jnp.ones((n, NB), jnp.float32)
    for i in range(n):
        here = rows == i
        pivot = jnp.broadcast_to(cols[i][i : i + 1, :], (n, NB))
        scale = 1.0 / pivot
        pivots = jnp.where(here, pivot, pivots)
        lift = jnp.where(here, 0.0, cols[i] * scale)
        for j in range(i + 1, n):
            cols[j] = cols[j] - lift * jnp.broadcast_to(cols[j][i : i + 1, :], (n, NB))
        upper = [jnp.where(here, p, u) for p, u in zip(parts, upper)]
        parts = [p - lift * jnp.broadcast_to(p[i : i + 1, :], (n, NB)) for p in parts]
    root = lax.rsqrt(pivots)
    inverse = 1.0 / pivots
    upper = jnp.concatenate([u * root for u in upper], axis=1)
    solved = jnp.concatenate([p * inverse for p in parts], axis=1)
    return upper, solved


def factor_kernel(lead_ref, inv_ref, low_ref, work, upper):
    eye = lax.broadcasted_iota(jnp.int32, (NB, NB), 0) == lax.broadcasted_iota(jnp.int32, (NB, NB), 1)
    eye = eye.astype(jnp.float32)
    zero = jnp.zeros((NB, NB), jnp.float32)

    def tile(core, n):
        return lead_ref[core, :, n * PART : (n + 1) * PART, :].reshape(NB, NB)

    rows = ((tile(0, 0), tile(1, 0), tile(0, 1)), (tile(1, 1), tile(1, 2).T, zero), (tile(0, 2), zero, zero))
    for k, tiles in enumerate(rows):
        for q, value in zip((0, 2, 3), tiles):
            work[k, :, q * NB : (q + 1) * NB] = value
        work[k, :, NB : 2 * NB] = eye

    def panel(k, carry):
        strip = work[k, 0:STRIP, :]
        for b in range(NB // STRIP):
            first = b * STRIP
            rows_u, solved = factor_strip(strip, first)
            upper[first : first + STRIP, :] = rows_u
            rest = NB - first - STRIP
            if rest:
                pieces = [jnp.zeros((first, 4 * NB), jnp.float32)] if first else []
                pieces += [solved, jnp.zeros((rest, 4 * NB), jnp.float32)]
                padded = jnp.concatenate(pieces, axis=0)
                strip = work[k, first + STRIP : first + 2 * STRIP, :]
                strip = strip - mm3(strip[:, :NB], padded)
                if rest > STRIP:
                    below = work[k, first + 2 * STRIP :, :]
                    work[k, first + 2 * STRIP :, :] = below - mm3(below[:, :NB], padded)
        inv_ref[k] = upper[:, NB : 2 * NB]

        @pl.when(k < PANELS - 1)
        def _():
            u1 = upper[:, 2 * NB : 3 * NB]
            u2 = upper[:, 3 * NB :]
            l1 = u1.T
            l2 = u2.T
            low_ref[k, 0] = l1
            low_ref[k, 1] = l2
            work[k + 1, :, :NB] -= mm(l1, u1)
            work[k + 1, :, 2 * NB : 3 * NB] -= mm(l1, u2)
            work[k + 2, :, :NB] -= mm(l2, u2)

        return carry

    lax.fori_loop(0, PANELS, panel, 0)


def factor(lead):
    return pl.pallas_call(
        factor_kernel,
        out_shape=(
            jax.ShapeDtypeStruct((PANELS, NB, NB), jnp.float32),
            jax.ShapeDtypeStruct((PANELS - 1, 2, NB, NB), jnp.float32),
        ),
        in_specs=[VMEM],
        out_specs=[VMEM, VMEM],
        scratch_shapes=[
            pltpu.VMEM((PANELS + 1, NB, 4 * NB), jnp.float32),
            pltpu.VMEM((NB, 4 * NB), jnp.float32),
        ],
        name="factor",
    )(lead)


def mm3_nt(a, b):
    return mm3(a, b, (1, 1))


def pack_cols_kernel(got_ref, cols_ref):
    size = got_ref.shape[1] - 2 * PART
    for i in range(PANELS):
        tile = got_ref[i, 2 * PART :, :]
        for z in range(NZ):
            cols_ref[z, i * size : (i + 1) * size, :] = tile


def pack(kernel, got, rows):
    return pl.pallas_call(
        kernel, out_shape=jax.ShapeDtypeStruct((NZ, rows, NB), jnp.float32), in_specs=[VMEM], out_specs=VMEM
    )(got)


def finish_kernel(inv_ref, low_ref, mine_ref, other_ref, y_ref, m_ref, out_ref, x_got):
    my_row = lax.axis_index("row")
    my_col = lax.axis_index("col")
    col_count = lax.axis_size("col")
    row_count = NX * NZ
    core = lax.rem(my_col, 2)
    odd = lax.rem(my_col // 2, 2)
    x_got[core] = mine_ref[...]
    x_got[1 - core] = other_ref[...]
    left = [x_got[0, odd], x_got[1, odd], x_got[0, 1 - odd]]
    rows0 = mm3_nt(left[0], inv_ref[0])
    rows1 = mm3_nt(left[1] - mm3_nt(rows0, low_ref[0, 0]), inv_ref[1])
    rows2 = mm3_nt(left[2] - mm3_nt(rows0, low_ref[0, 1]) - mm3_nt(rows1, low_ref[1, 0]), inv_ref[2])
    right = []
    for i in range(PANELS):
        tiles = []
        for s in range(4):
            at = i * PART * 4 + s
            tiles.append(jnp.concatenate([y_ref[z, pl.ds(at, PART, stride=4), :] for z in range(NZ)], axis=0))
        right.append(jnp.concatenate(tiles, axis=1))
    cols0 = mm3(inv_ref[0], right[0])
    cols1 = mm3(inv_ref[1], right[1] - mm3(low_ref[0, 0], cols0))
    cols2 = mm3(inv_ref[2], right[2] - mm3(low_ref[0, 1], cols0) - mm3(low_ref[1, 0], cols1))
    rows = jnp.concatenate([rows0, rows1, rows2], axis=1)
    cols = jnp.concatenate([cols0, cols1, cols2], axis=0)
    panel = jnp.where(my_col == 0, rows0, jnp.where(my_col == 1, rows1, rows2))
    u = lax.broadcasted_iota(jnp.int32, (NB, NB), 0)
    v = lax.broadcasted_iota(jnp.int32, (NB, NB), 1)
    for t in range(2):
        live = min(4, -(-(t + 1) * row_count // col_count))
        product = mm3(rows[t * NB : (t + 1) * NB], cols[:, : live * NB])
        for s in range(4):
            if s >= live:
                out_ref[t, pl.ds(s, NB, stride=4), :] = jnp.zeros((NB, NB), jnp.float32)
                continue
            value = m_ref[t, pl.ds(s, NB, stride=4), :] - product[:, s * NB : (s + 1) * NB]
            if s == 0:
                value = jnp.where(my_col < PANELS, panel[t * NB : (t + 1) * NB], value)
            below = (t * row_count + my_row - s * col_count - my_col) * NB
            out_ref[t, pl.ds(s, NB, stride=4), :] = jnp.where(below + u >= v, value, 0.0)


def finish(inverse, low, mine, other, y_part, matrix):
    return pl.pallas_call(
        finish_kernel,
        out_shape=jax.ShapeDtypeStruct(matrix.shape, jnp.float32),
        in_specs=[VMEM] * 6,
        out_specs=VMEM,
        scratch_shapes=[pltpu.VMEM((2,) + mine.shape, jnp.float32)],
        name="finish",
    )(inverse, low, mine, other, y_part, matrix)


def to_all(value, axis, groups):
    count = len(groups[0])
    return lax.all_to_all(jnp.broadcast_to(value[None], (count,) + value.shape), axis, 0, 0, axis_index_groups=groups)


def per_device(covariance):
    tile_rows, nb, tile_cols, _ = covariance.shape
    col_count = lax.axis_size("col")
    my_col = lax.axis_index("col")
    matrix = covariance.reshape(tile_rows, nb * tile_cols, nb)
    along_z = [[z * NX + x for z in range(NZ)] for x in range(NX)]
    along_x = [[z * NX + x for x in range(NX)] for z in range(NZ)]
    along_y = [[c for c in range(q, col_count, 2)] for q in range(2)]
    pairs = [[c, c + 1] for c in range(0, col_count, 2)]
    half, quarter = col_count // 2, col_count // 4

    mine = covariance[:, :, 0, :].reshape(tile_rows * nb, nb)
    far = lax.ppermute(mine, "col", [(c, c + half) for c in range(PANELS)])
    mine = jnp.where(my_col >= half, far, mine)
    mid = lax.ppermute(mine, "col", [(c + h, c + h + quarter) for c in range(PANELS) for h in (0, half)])
    mine = jnp.where(my_col % half >= quarter, mid, mine)
    steps = []
    for start in range(0, col_count, quarter):
        steps += [(start, start + 2), (start + 1, start + 3), (start + 2, start)]
    near = lax.ppermute(mine, "col", steps)
    panels = jnp.stack([mine, near])
    other = lax.ppermute(panels, "col", [(c, c ^ 1) for c in range(col_count)])

    piece = lax.all_to_all(matrix[0].reshape(NZ, PART * tile_cols, nb), "row", 0, 0, axis_index_groups=along_z)[0]
    head = piece.reshape(PART, tile_cols, nb)[:, 0, :]
    own = to_all(head, "col", along_y)[:2]
    got = to_all(jnp.concatenate([own.reshape(2 * PART, nb), piece], axis=0), "row", along_x)
    first_core = my_col % 2 == 0
    lead = [
        got[0, :PART],
        jnp.where(first_core, got[0, PART : 2 * PART], got[1, :PART]),
        jnp.where(first_core, got[2, PART : 2 * PART], got[2, :PART]),
    ]
    lead = jnp.concatenate(lead, axis=0)
    lead = to_all(lead, "row", along_z)
    lead = lax.all_gather(lead, "col", axis_index_groups=pairs)
    cols = pack(pack_cols_kernel, got, PANELS * PART * tile_cols)
    y_part = lax.all_to_all(cols, "row", 0, 0, axis_index_groups=along_z)
    inverse, low = factor(lead)
    out = finish(inverse, low, panels, other, y_part, matrix)
    return out.reshape(covariance.shape)


def solution(mesh):
    placed = (P(None, "row", None, "col"),)
    return jax.shard_map(
        per_device,
        mesh=mesh,
        in_specs=placed,
        out_specs=P(None, "row", None, "col"),
        check_vma=False,
    )
```

```python
import jax
import jax.numpy as jnp
from jax import lax
from jax.experimental import pallas as pl
from jax.experimental.pallas import tpu as pltpu
from jax.sharding import PartitionSpec as P


NB = 128
PANELS = 3
STRIP = 16
NX = 4
NZ = 8
PART = NB // NZ
VMEM = pl.BlockSpec(memory_space=pltpu.VMEM)
SMEM = pl.BlockSpec(memory_space=pltpu.SMEM)


def mm(a, b):
    return jnp.dot(a, b, precision=lax.Precision.HIGHEST, preferred_element_type=jnp.float32)


def mm3(a, b, contract=(1, 0)):
    a_high, b_high = a.astype(jnp.bfloat16), b.astype(jnp.bfloat16)
    a_low = (a - a_high.astype(jnp.float32)).astype(jnp.bfloat16)
    b_low = (b - b_high.astype(jnp.float32)).astype(jnp.bfloat16)
    dims = (((contract[0],), (contract[1],)), ((), ()))

    def dot(p, q):
        return lax.dot_general(p, q, dims, preferred_element_type=jnp.float32)

    return dot(a_high, b_high) + (dot(a_high, b_low) + dot(a_low, b_high))


def factor_strip(strip, first):
    n = strip.shape[0]
    rows = lax.broadcasted_iota(jnp.int32, (n, NB), 0)
    cols = [jnp.broadcast_to(strip[:, first + i : first + i + 1], (n, NB)) for i in range(n)]
    parts = [strip[:, q * NB : (q + 1) * NB] for q in range(strip.shape[1] // NB)]
    upper = list(parts)
    pivots = jnp.ones((n, NB), jnp.float32)
    for i in range(n):
        here = rows == i
        pivot = jnp.broadcast_to(cols[i][i : i + 1, :], (n, NB))
        scale = 1.0 / pivot
        pivots = jnp.where(here, pivot, pivots)
        lift = jnp.where(here, 0.0, cols[i] * scale)
        for j in range(i + 1, n):
            cols[j] = cols[j] - lift * jnp.broadcast_to(cols[j][i : i + 1, :], (n, NB))
        upper = [jnp.where(here, p, u) for p, u in zip(parts, upper)]
        parts = [p - lift * jnp.broadcast_to(p[i : i + 1, :], (n, NB)) for p in parts]
    root = lax.rsqrt(pivots)
    inverse = 1.0 / pivots
    upper = jnp.concatenate([u * root for u in upper], axis=1)
    solved = jnp.concatenate([p * inverse for p in parts], axis=1)
    return upper, solved


def factor_kernel(got_ref, inv_ref, low_ref, rows_ref, work, upper):
    eye = lax.broadcasted_iota(jnp.int32, (NB, NB), 0) == lax.broadcasted_iota(jnp.int32, (NB, NB), 1)
    eye = eye.astype(jnp.float32)
    zero = jnp.zeros((NB, NB), jnp.float32)

    def tile(core, n):
        starts = [(z * PANELS + n) * PART for z in range(NZ)]
        return jnp.concatenate([got_ref[core, at : at + PART, :] for at in starts], axis=0)

    rows = ((tile(0, 0), tile(1, 0), tile(0, 1)), (tile(1, 1), tile(1, 2).T, zero), (tile(0, 2), zero, zero))
    for k, tiles in enumerate(rows):
        for q, value in zip((0, 2, 3), tiles):
            work[k, :, q * NB : (q + 1) * NB] = value
        work[k, :, NB : 2 * NB] = eye

    def panel(k, carry):
        strip = work[k, 0:STRIP, :]
        for b in range(NB // STRIP):
            first = b * STRIP
            rows_u, solved = factor_strip(strip, first)
            upper[first : first + STRIP, :] = rows_u
            rest = NB - first - STRIP
            if rest:
                pieces = [jnp.zeros((first, 4 * NB), jnp.float32)] if first else []
                pieces += [solved, jnp.zeros((rest, 4 * NB), jnp.float32)]
                padded = jnp.concatenate(pieces, axis=0)
                strip = work[k, first + STRIP : first + 2 * STRIP, :]
                strip = strip - mm3(strip[:, :NB], padded)
                if rest > STRIP:
                    below = work[k, first + 2 * STRIP :, :]
                    work[k, first + 2 * STRIP :, :] = below - mm3(below[:, :NB], padded)
        inv_ref[k] = upper[:, NB : 2 * NB]

        @pl.when(k < PANELS - 1)
        def _():
            u1 = upper[:, 2 * NB : 3 * NB]
            u2 = upper[:, 3 * NB :]
            l1 = u1.T
            l2 = u2.T
            low_ref[k, 0] = l1
            low_ref[k, 1] = l2
            work[k + 1, :, :NB] -= mm(l1, u1)
            work[k + 1, :, 2 * NB : 3 * NB] -= mm(l1, u2)
            work[k + 2, :, :NB] -= mm(l2, u2)

        return carry

    lax.fori_loop(0, PANELS, panel, 0)

    odd = lax.rem(lax.axis_index("col") // 2, 2)

    def row_panel(core, near):
        at = pl.multiple_of(NZ * PANELS * PART + near * 2 * NB, NB)
        return got_ref[core, pl.ds(at, 2 * NB), :]

    left = [row_panel(0, odd), row_panel(1, odd), row_panel(0, 1 - odd)]
    rows0 = mm3_nt(left[0], inv_ref[0])
    rows1 = mm3_nt(left[1] - mm3_nt(rows0, low_ref[0, 0]), inv_ref[1])
    rows2 = mm3_nt(left[2] - mm3_nt(rows0, low_ref[0, 1]) - mm3_nt(rows1, low_ref[1, 0]), inv_ref[2])
    for k, value in enumerate((rows0, rows1, rows2)):
        rows_ref[:, k * NB : (k + 1) * NB] = value


def factor(got):
    return pl.pallas_call(
        factor_kernel,
        out_shape=(
            jax.ShapeDtypeStruct((PANELS, NB, NB), jnp.float32),
            jax.ShapeDtypeStruct((PANELS - 1, 2, NB, NB), jnp.float32),
            jax.ShapeDtypeStruct((2 * NB, PANELS * NB), jnp.float32),
        ),
        in_specs=[VMEM],
        out_specs=[VMEM] * 3,
        scratch_shapes=[
            pltpu.VMEM((PANELS + 1, NB, 4 * NB), jnp.float32),
            pltpu.VMEM((NB, 4 * NB), jnp.float32),
        ],
        name="factor",
    )(got)


def mm3_nt(a, b):
    return mm3(a, b, (1, 1))


def pack_cols_kernel(got_ref, cols_ref):
    size = got_ref.shape[1] - 2 * PART
    for i in range(PANELS):
        tile = got_ref[i, 2 * PART :, :]
        for z in range(NZ):
            cols_ref[z, i * size : (i + 1) * size, :] = tile


def pack(kernel, got, rows):
    return pl.pallas_call(
        kernel, out_shape=jax.ShapeDtypeStruct((NZ, rows, NB), jnp.float32), in_specs=[VMEM], out_specs=VMEM
    )(got)


def finish_kernel(inv_ref, low_ref, rows_ref, y_ref, m_ref, out_ref):
    my_row = lax.axis_index("row")
    my_col = lax.axis_index("col")
    col_count = lax.axis_size("col")
    row_count = NX * NZ
    rows = rows_ref[...]
    right = []
    for i in range(PANELS):
        tiles = []
        for s in range(4):
            at = i * PART * 4 + s
            tiles.append(jnp.concatenate([y_ref[z, pl.ds(at, PART, stride=4), :] for z in range(NZ)], axis=0))
        right.append(jnp.concatenate(tiles, axis=1))
    cols0 = mm3(inv_ref[0], right[0])
    cols1 = mm3(inv_ref[1], right[1] - mm3(low_ref[0, 0], cols0))
    cols2 = mm3(inv_ref[2], right[2] - mm3(low_ref[0, 1], cols0) - mm3(low_ref[1, 0], cols1))
    cols = jnp.concatenate([cols0, cols1, cols2], axis=0)
    parts = [rows[:, k * NB : (k + 1) * NB] for k in range(PANELS)]
    panel = jnp.where(my_col == 0, parts[0], jnp.where(my_col == 1, parts[1], parts[2]))
    u = lax.broadcasted_iota(jnp.int32, (NB, NB), 0)
    v = lax.broadcasted_iota(jnp.int32, (NB, NB), 1)
    for t in range(2):
        live = min(4, -(-(t + 1) * row_count // col_count))
        product = mm3(rows[t * NB : (t + 1) * NB], cols[:, : live * NB])
        for s in range(4):
            if s >= live:
                out_ref[t, pl.ds(s, NB, stride=4), :] = jnp.zeros((NB, NB), jnp.float32)
                continue
            value = m_ref[t, pl.ds(s, NB, stride=4), :] - product[:, s * NB : (s + 1) * NB]
            if s == 0:
                value = jnp.where(my_col < PANELS, panel[t * NB : (t + 1) * NB], value)
            below = (t * row_count + my_row - s * col_count - my_col) * NB
            out_ref[t, pl.ds(s, NB, stride=4), :] = jnp.where(below + u >= v, value, 0.0)


def finish(inverse, low, rows, y_part, matrix):
    return pl.pallas_call(
        finish_kernel,
        out_shape=jax.ShapeDtypeStruct(matrix.shape, jnp.float32),
        in_specs=[VMEM] * 5,
        out_specs=VMEM,
        name="finish",
    )(inverse, low, rows, y_part, matrix)


def to_all(value, axis, groups):
    count = len(groups[0])
    return lax.all_to_all(jnp.broadcast_to(value[None], (count,) + value.shape), axis, 0, 0, axis_index_groups=groups)


def per_device(covariance):
    tile_rows, nb, tile_cols, _ = covariance.shape
    col_count = lax.axis_size("col")
    my_col = lax.axis_index("col")
    matrix = covariance.reshape(tile_rows, nb * tile_cols, nb)
    along_z = [[z * NX + x for z in range(NZ)] for x in range(NX)]
    along_x = [[z * NX + x for x in range(NX)] for z in range(NZ)]
    along_y = [[c for c in range(q, col_count, 2)] for q in range(2)]
    pairs = [[c, c + 1] for c in range(0, col_count, 2)]
    half, quarter = col_count // 2, col_count // 4

    mine = covariance[:, :, 0, :].reshape(tile_rows * nb, nb)
    far = lax.ppermute(mine, "col", [(c, c + half) for c in range(PANELS)])
    mine = jnp.where(my_col >= half, far, mine)
    mid = lax.ppermute(mine, "col", [(c + h, c + h + quarter) for c in range(PANELS) for h in (0, half)])
    mine = jnp.where(my_col % half >= quarter, mid, mine)
    steps = []
    for start in range(0, col_count, quarter):
        steps += [(start, start + 2), (start + 1, start + 3), (start + 2, start)]
    near = lax.ppermute(mine, "col", steps)
    piece = lax.all_to_all(matrix[0].reshape(NZ, PART * tile_cols, nb), "row", 0, 0, axis_index_groups=along_z)[0]
    head = piece.reshape(PART, tile_cols, nb)[:, 0, :]
    own = to_all(head, "col", along_y)[:2]
    got = to_all(jnp.concatenate([own.reshape(2 * PART, nb), piece], axis=0), "row", along_x)
    first_core = my_col % 2 == 0
    lead = [
        got[0, :PART],
        jnp.where(first_core, got[0, PART : 2 * PART], got[1, :PART]),
        jnp.where(first_core, got[2, PART : 2 * PART], got[2, :PART]),
    ]
    lead = jnp.concatenate(lead, axis=0)
    lead = to_all(lead, "row", along_z)
    sent = jnp.concatenate([lead.reshape(NZ * PANELS * PART, nb), mine, near], axis=0)
    gathered = lax.all_gather(sent, "col", axis_index_groups=pairs)
    cols = pack(pack_cols_kernel, got, PANELS * PART * tile_cols)
    y_part = lax.all_to_all(cols, "row", 0, 0, axis_index_groups=along_z)
    inverse, low, rows = factor(gathered)
    out = finish(inverse, low, rows, y_part, matrix)
    return out.reshape(covariance.shape)


def solution(mesh):
    placed = (P(None, "row", None, "col"),)
    return jax.shard_map(
        per_device,
        mesh=mesh,
        in_specs=placed,
        out_specs=P(None, "row", None, "col"),
        check_vma=False,
    )
```

```python
import jax
import jax.numpy as jnp
from jax import lax
from jax.experimental import pallas as pl
from jax.experimental.pallas import tpu as pltpu
from jax.sharding import PartitionSpec as P


NB = 128
PANELS = 3
STRIP = 16
NX = 4
NZ = 8
PART = NB // NZ
VMEM = pl.BlockSpec(memory_space=pltpu.VMEM)
SMEM = pl.BlockSpec(memory_space=pltpu.SMEM)


def mm3(a, b, contract=(1, 0)):
    a_high, b_high = a.astype(jnp.bfloat16), b.astype(jnp.bfloat16)
    a_low = (a - a_high.astype(jnp.float32)).astype(jnp.bfloat16)
    b_low = (b - b_high.astype(jnp.float32)).astype(jnp.bfloat16)
    dims = (((contract[0],), (contract[1],)), ((), ()))

    def dot(p, q):
        return lax.dot_general(p, q, dims, preferred_element_type=jnp.float32)

    return dot(a_high, b_high) + (dot(a_high, b_low) + dot(a_low, b_high))


def factor_strip(strip, first):
    n = strip.shape[0]
    rows = lax.broadcasted_iota(jnp.int32, (n, NB), 0)
    cols = [jnp.broadcast_to(strip[:, first + i : first + i + 1], (n, NB)) for i in range(n)]
    parts = [strip[:, q * NB : (q + 1) * NB] for q in range(strip.shape[1] // NB)]
    upper = list(parts)
    pivots = jnp.ones((n, NB), jnp.float32)
    for i in range(n):
        here = rows == i
        pivot = jnp.broadcast_to(cols[i][i : i + 1, :], (n, NB))
        scale = 1.0 / pivot
        pivots = jnp.where(here, pivot, pivots)
        lift = jnp.where(here, 0.0, cols[i] * scale)
        for j in range(i + 1, n):
            cols[j] = cols[j] - lift * jnp.broadcast_to(cols[j][i : i + 1, :], (n, NB))
        upper = [jnp.where(here, p, u) for p, u in zip(parts, upper)]
        parts = [p - lift * jnp.broadcast_to(p[i : i + 1, :], (n, NB)) for p in parts]
    root = lax.rsqrt(pivots)
    inverse = 1.0 / pivots
    upper = jnp.concatenate([u * root for u in upper], axis=1)
    solved = jnp.concatenate([p * inverse for p in parts], axis=1)
    return upper, solved


def factor_kernel(got_ref, panel_ref, gain_ref, inv_ref, low_ref, work, upper):
    eye = lax.broadcasted_iota(jnp.int32, (NB, NB), 0) == lax.broadcasted_iota(jnp.int32, (NB, NB), 1)
    eye = eye.astype(jnp.float32)
    zero = jnp.zeros((NB, NB), jnp.float32)

    def tile(core, n):
        starts = [(z * PANELS + n) * PART for z in range(NZ)]
        return jnp.concatenate([got_ref[core, at : at + PART, :] for at in starts], axis=0)

    rows = ((tile(0, 0), tile(1, 0), tile(0, 1)), (tile(1, 1), tile(1, 2).T, zero), (tile(0, 2), zero, zero))
    for k, tiles in enumerate(rows):
        for q, value in zip((0, 2, 3), tiles):
            work[k, :, q * NB : (q + 1) * NB] = value
        work[k, :, NB : 2 * NB] = eye

    def panel(k, carry):
        strip = work[k, 0:STRIP, :]
        for b in range(NB // STRIP):
            first = b * STRIP
            rows_u, solved = factor_strip(strip, first)
            upper[first : first + STRIP, :] = rows_u
            rest = NB - first - STRIP
            if rest:
                pieces = [jnp.zeros((first, 4 * NB), jnp.float32)] if first else []
                pieces += [solved, jnp.zeros((rest, 4 * NB), jnp.float32)]
                padded = jnp.concatenate(pieces, axis=0)
                strip = work[k, first + STRIP : first + 2 * STRIP, :]
                strip = strip - mm3(strip[:, :NB], padded)
                if rest > STRIP:
                    below = work[k, first + 2 * STRIP :, :]
                    work[k, first + 2 * STRIP :, :] = below - mm3(below[:, :NB], padded)
        inv_ref[k] = upper[:, NB : 2 * NB]

        @pl.when(k < PANELS - 1)
        def _():
            u1 = upper[:, 2 * NB : 3 * NB]
            u2 = upper[:, 3 * NB :]
            l1 = u1.T
            l2 = u2.T
            low_ref[k, 0] = l1
            low_ref[k, 1] = l2
            work[k + 1, :, :NB] -= mm3(l1, u1)
            work[k + 1, :, 2 * NB : 3 * NB] -= mm3(l1, u2)
            work[k + 2, :, :NB] -= mm3(l2, u2)

        return carry

    lax.fori_loop(0, PANELS, panel, 0)

    odd = lax.rem(lax.axis_index("col") // 2, 2)

    def row_panel(core, near):
        at = pl.multiple_of(NZ * PANELS * PART + near * 2 * NB, NB)
        return got_ref[core, pl.ds(at, 2 * NB), :]

    left = [row_panel(0, odd), row_panel(1, odd), row_panel(0, 1 - odd)]
    rows0 = mm3_nt(left[0], inv_ref[0])
    rows1 = mm3_nt(left[1] - mm3_nt(rows0, low_ref[0, 0]), inv_ref[1])
    rows2 = mm3_nt(left[2] - mm3_nt(rows0, low_ref[0, 1]) - mm3_nt(rows1, low_ref[1, 0]), inv_ref[2])
    my_col = lax.axis_index("col")
    panel_ref[...] = jnp.where(my_col == 0, rows0, jnp.where(my_col == 1, rows1, rows2))
    gain2 = mm3(rows2, inv_ref[2])
    gain1 = mm3(rows1 - mm3(gain2, low_ref[1, 0]), inv_ref[1])
    gain0 = mm3(rows0 - mm3(gain1, low_ref[0, 0]) - mm3(gain2, low_ref[0, 1]), inv_ref[0])
    for k, value in enumerate((gain0, gain1, gain2)):
        gain_ref[:, k * NB : (k + 1) * NB] = value


def factor(got):
    return pl.pallas_call(
        factor_kernel,
        out_shape=(
            jax.ShapeDtypeStruct((2 * NB, NB), jnp.float32),
            jax.ShapeDtypeStruct((2 * NB, PANELS * NB), jnp.float32),
        ),
        in_specs=[VMEM],
        out_specs=[VMEM] * 2,
        scratch_shapes=[
            pltpu.VMEM((PANELS, NB, NB), jnp.float32),
            pltpu.VMEM((PANELS - 1, 2, NB, NB), jnp.float32),
            pltpu.VMEM((PANELS + 1, NB, 4 * NB), jnp.float32),
            pltpu.VMEM((NB, 4 * NB), jnp.float32),
        ],
        name="factor",
    )(got)


def mm3_nt(a, b):
    return mm3(a, b, (1, 1))


def pack_cols_kernel(got_ref, cols_ref):
    size = got_ref.shape[1] - 2 * PART
    for i in range(PANELS):
        tile = got_ref[i, 2 * PART :, :]
        for z in range(NZ):
            cols_ref[z, i * size : (i + 1) * size, :] = tile


def pack(kernel, got, rows):
    return pl.pallas_call(
        kernel, out_shape=jax.ShapeDtypeStruct((NZ, rows, NB), jnp.float32), in_specs=[VMEM], out_specs=VMEM
    )(got)


def finish_kernel(panel_ref, gain_ref, y_ref, m_ref, out_ref):
    my_row = lax.axis_index("row")
    my_col = lax.axis_index("col")
    col_count = lax.axis_size("col")
    row_count = NX * NZ
    gain = gain_ref[...]
    right = []
    for i in range(PANELS):
        tiles = []
        for s in range(4):
            at = i * PART * 4 + s
            tiles.append(jnp.concatenate([y_ref[z, pl.ds(at, PART, stride=4), :] for z in range(NZ)], axis=0))
        right.append(jnp.concatenate(tiles, axis=1))
    cols = jnp.concatenate(right, axis=0)
    u = lax.broadcasted_iota(jnp.int32, (NB, NB), 0)
    v = lax.broadcasted_iota(jnp.int32, (NB, NB), 1)
    for t in range(2):
        live = min(4, -(-(t + 1) * row_count // col_count))
        product = mm3(gain[t * NB : (t + 1) * NB], cols[:, : live * NB])
        for s in range(4):
            if s >= live:
                out_ref[t, pl.ds(s, NB, stride=4), :] = jnp.zeros((NB, NB), jnp.float32)
                continue
            value = m_ref[t, pl.ds(s, NB, stride=4), :] - product[:, s * NB : (s + 1) * NB]
            if s == 0:
                value = jnp.where(my_col < PANELS, panel_ref[t * NB : (t + 1) * NB, :], value)
            below = (t * row_count + my_row - s * col_count - my_col) * NB
            out_ref[t, pl.ds(s, NB, stride=4), :] = jnp.where(below + u >= v, value, 0.0)


def finish(panel, gain, y_part, matrix):
    return pl.pallas_call(
        finish_kernel,
        out_shape=jax.ShapeDtypeStruct(matrix.shape, jnp.float32),
        in_specs=[VMEM] * 4,
        out_specs=VMEM,
        name="finish",
    )(panel, gain, y_part, matrix)


def to_all(value, axis, groups):
    count = len(groups[0])
    return lax.all_to_all(jnp.broadcast_to(value[None], (count,) + value.shape), axis, 0, 0, axis_index_groups=groups)


def per_device(covariance):
    tile_rows, nb, tile_cols, _ = covariance.shape
    col_count = lax.axis_size("col")
    my_col = lax.axis_index("col")
    matrix = covariance.reshape(tile_rows, nb * tile_cols, nb)
    along_z = [[z * NX + x for z in range(NZ)] for x in range(NX)]
    along_x = [[z * NX + x for x in range(NX)] for z in range(NZ)]
    along_y = [[c for c in range(q, col_count, 2)] for q in range(2)]
    pairs = [[c, c + 1] for c in range(0, col_count, 2)]
    half, quarter = col_count // 2, col_count // 4

    mine = covariance[:, :, 0, :].reshape(tile_rows * nb, nb)
    far = lax.ppermute(mine, "col", [(c, c + half) for c in range(PANELS)])
    mine = jnp.where(my_col >= half, far, mine)
    mid = lax.ppermute(mine, "col", [(c + h, c + h + quarter) for c in range(PANELS) for h in (0, half)])
    mine = jnp.where(my_col % half >= quarter, mid, mine)
    steps = []
    for start in range(0, col_count, quarter):
        steps += [(start, start + 2), (start + 1, start + 3), (start + 2, start)]
    near = lax.ppermute(mine, "col", steps)
    piece = lax.all_to_all(matrix[0].reshape(NZ, PART * tile_cols, nb), "row", 0, 0, axis_index_groups=along_z)[0]
    head = piece.reshape(PART, tile_cols, nb)[:, 0, :]
    own = to_all(head, "col", along_y)[:2]
    got = to_all(jnp.concatenate([own.reshape(2 * PART, nb), piece], axis=0), "row", along_x)
    first_core = my_col % 2 == 0
    lead = [
        got[0, :PART],
        jnp.where(first_core, got[0, PART : 2 * PART], got[1, :PART]),
        jnp.where(first_core, got[2, PART : 2 * PART], got[2, :PART]),
    ]
    lead = jnp.concatenate(lead, axis=0)
    lead = to_all(lead, "row", along_z)
    sent = jnp.concatenate([lead.reshape(NZ * PANELS * PART, nb), mine, near], axis=0)
    gathered = lax.all_gather(sent, "col", axis_index_groups=pairs)
    cols = pack(pack_cols_kernel, got, PANELS * PART * tile_cols)
    y_part = lax.all_to_all(cols, "row", 0, 0, axis_index_groups=along_z)
    panel, gain = factor(gathered)
    out = finish(panel, gain, y_part, matrix)
    return out.reshape(covariance.shape)


def solution(mesh):
    placed = (P(None, "row", None, "col"),)
    return jax.shard_map(
        per_device,
        mesh=mesh,
        in_specs=placed,
        out_specs=P(None, "row", None, "col"),
        check_vma=False,
    )
```

```python
import jax
import jax.numpy as jnp
from jax import lax
from jax.experimental import pallas as pl
from jax.experimental.pallas import tpu as pltpu
from jax.sharding import PartitionSpec as P


NB = 128
PANELS = 3
STRIP = 16
NX = 4
NZ = 8
PART = NB // NZ
VMEM = pl.BlockSpec(memory_space=pltpu.VMEM)
SMEM = pl.BlockSpec(memory_space=pltpu.SMEM)


def mm3(a, b, contract=(1, 0)):
    a_high, b_high = a.astype(jnp.bfloat16), b.astype(jnp.bfloat16)
    a_low = (a - a_high.astype(jnp.float32)).astype(jnp.bfloat16)
    b_low = (b - b_high.astype(jnp.float32)).astype(jnp.bfloat16)
    dims = (((contract[0],), (contract[1],)), ((), ()))

    def dot(p, q):
        return lax.dot_general(p, q, dims, preferred_element_type=jnp.float32)

    return dot(a_high, b_high) + (dot(a_high, b_low) + dot(a_low, b_high))


def factor_strip(strip, first):
    n = strip.shape[0]
    rows = lax.broadcasted_iota(jnp.int32, (n, NB), 0)
    cols = [jnp.broadcast_to(strip[:, first + i : first + i + 1], (n, NB)) for i in range(n)]
    parts = [strip[:, q * NB : (q + 1) * NB] for q in range(strip.shape[1] // NB)]
    upper = list(parts)
    pivots = jnp.ones((n, NB), jnp.float32)
    for i in range(n):
        here = rows == i
        pivot = jnp.broadcast_to(cols[i][i : i + 1, :], (n, NB))
        scale = 1.0 / pivot
        pivots = jnp.where(here, pivot, pivots)
        lift = jnp.where(here, 0.0, cols[i] * scale)
        for j in range(i + 1, n):
            cols[j] = cols[j] - lift * jnp.broadcast_to(cols[j][i : i + 1, :], (n, NB))
        upper = [jnp.where(here, p, u) for p, u in zip(parts, upper)]
        parts = [p - lift * jnp.broadcast_to(p[i : i + 1, :], (n, NB)) for p in parts]
    root = lax.rsqrt(pivots)
    inverse = 1.0 / pivots
    upper = jnp.concatenate([u * root for u in upper], axis=1)
    solved = jnp.concatenate([p * inverse for p in parts], axis=1)
    return upper, solved


def factor_kernel(got_ref, panel_ref, gain_ref, inv_ref, low_ref, work, upper):
    eye = lax.broadcasted_iota(jnp.int32, (NB, NB), 0) == lax.broadcasted_iota(jnp.int32, (NB, NB), 1)
    eye = eye.astype(jnp.float32)
    zero = jnp.zeros((NB, NB), jnp.float32)

    def tile(core, n):
        starts = [(z * PANELS + n) * PART for z in range(NZ)]
        return jnp.concatenate([got_ref[core, at : at + PART, :] for at in starts], axis=0)

    rows = ((tile(0, 0), tile(1, 0), tile(0, 1)), (tile(1, 1), tile(1, 2).T, zero), (tile(0, 2), zero, zero))
    for k, tiles in enumerate(rows):
        for q, value in zip((0, 2, 3), tiles):
            work[k, :, q * NB : (q + 1) * NB] = value
        work[k, :, NB : 2 * NB] = eye

    odd = lax.rem(lax.axis_index("col") // 2, 2)

    def row_panel(core, near):
        at = pl.multiple_of(NZ * PANELS * PART + near * 2 * NB, NB)
        return got_ref[core, pl.ds(at, 2 * NB), :]

    left = [row_panel(0, odd), row_panel(1, odd), row_panel(0, 1 - odd)]
    rows = []
    for k in range(PANELS):
        strip = work[k, 0:STRIP, :]
        for b in range(NB // STRIP):
            first = b * STRIP
            rows_u, solved = factor_strip(strip, first)
            upper[first : first + STRIP, :] = rows_u
            rest = NB - first - STRIP
            if rest:
                pieces = [jnp.zeros((first, 4 * NB), jnp.float32)] if first else []
                pieces += [solved, jnp.zeros((rest, 4 * NB), jnp.float32)]
                padded = jnp.concatenate(pieces, axis=0)
                strip = work[k, first + STRIP : first + 2 * STRIP, :]
                strip = strip - mm3(strip[:, :NB], padded)
                if rest > STRIP:
                    below = work[k, first + 2 * STRIP :, :]
                    work[k, first + 2 * STRIP :, :] = below - mm3(below[:, :NB], padded)
        inv_ref[k] = upper[:, NB : 2 * NB]

        mine = left[k]
        for j in range(k):
            mine = mine - mm3_nt(rows[j], low_ref[j, k - j - 1])
        rows.append(mm3_nt(mine, inv_ref[k]))
        if k < PANELS - 1:
            u1 = upper[:, 2 * NB : 3 * NB]
            u2 = upper[:, 3 * NB :]
            l1 = u1.T
            l2 = u2.T
            low_ref[k, 0] = l1
            low_ref[k, 1] = l2
            work[k + 1, :, :NB] -= mm3(l1, u1)
            work[k + 1, :, 2 * NB : 3 * NB] -= mm3(l1, u2)
            work[k + 2, :, :NB] -= mm3(l2, u2)
    rows0, rows1, rows2 = rows
    my_col = lax.axis_index("col")
    panel_ref[...] = jnp.where(my_col == 0, rows0, jnp.where(my_col == 1, rows1, rows2))
    gain2 = mm3(rows2, inv_ref[2])
    gain1 = mm3(rows1 - mm3(gain2, low_ref[1, 0]), inv_ref[1])
    gain0 = mm3(rows0 - mm3(gain1, low_ref[0, 0]) - mm3(gain2, low_ref[0, 1]), inv_ref[0])
    for k, value in enumerate((gain0, gain1, gain2)):
        gain_ref[:, k * NB : (k + 1) * NB] = value


def factor(got):
    return pl.pallas_call(
        factor_kernel,
        out_shape=(
            jax.ShapeDtypeStruct((2 * NB, NB), jnp.float32),
            jax.ShapeDtypeStruct((2 * NB, PANELS * NB), jnp.float32),
        ),
        in_specs=[VMEM],
        out_specs=[VMEM] * 2,
        scratch_shapes=[
            pltpu.VMEM((PANELS, NB, NB), jnp.float32),
            pltpu.VMEM((PANELS - 1, 2, NB, NB), jnp.float32),
            pltpu.VMEM((PANELS + 1, NB, 4 * NB), jnp.float32),
            pltpu.VMEM((NB, 4 * NB), jnp.float32),
        ],
        name="factor",
    )(got)


def mm3_nt(a, b):
    return mm3(a, b, (1, 1))


def pack_cols_kernel(got_ref, cols_ref):
    size = got_ref.shape[1] - 2 * PART
    for i in range(PANELS):
        tile = got_ref[i, 2 * PART :, :]
        for z in range(NZ):
            cols_ref[z, i * size : (i + 1) * size, :] = tile


def pack(kernel, got, rows):
    return pl.pallas_call(
        kernel, out_shape=jax.ShapeDtypeStruct((NZ, rows, NB), jnp.float32), in_specs=[VMEM], out_specs=VMEM
    )(got)


def finish_kernel(panel_ref, gain_ref, y_ref, m_ref, out_ref):
    my_row = lax.axis_index("row")
    my_col = lax.axis_index("col")
    col_count = lax.axis_size("col")
    row_count = NX * NZ
    gain = gain_ref[...]
    right = []
    for i in range(PANELS):
        tiles = []
        for s in range(4):
            at = i * PART * 4 + s
            tiles.append(jnp.concatenate([y_ref[z, pl.ds(at, PART, stride=4), :] for z in range(NZ)], axis=0))
        right.append(jnp.concatenate(tiles, axis=1))
    cols = jnp.concatenate(right, axis=0)
    u = lax.broadcasted_iota(jnp.int32, (NB, NB), 0)
    v = lax.broadcasted_iota(jnp.int32, (NB, NB), 1)
    for t in range(2):
        live = min(4, -(-(t + 1) * row_count // col_count))
        product = mm3(gain[t * NB : (t + 1) * NB], cols[:, : live * NB])
        for s in range(4):
            if s >= live:
                out_ref[t, pl.ds(s, NB, stride=4), :] = jnp.zeros((NB, NB), jnp.float32)
                continue
            value = m_ref[t, pl.ds(s, NB, stride=4), :] - product[:, s * NB : (s + 1) * NB]
            if s == 0:
                value = jnp.where(my_col < PANELS, panel_ref[t * NB : (t + 1) * NB, :], value)
            below = (t * row_count + my_row - s * col_count - my_col) * NB
            out_ref[t, pl.ds(s, NB, stride=4), :] = jnp.where(below + u >= v, value, 0.0)


def finish(panel, gain, y_part, matrix):
    return pl.pallas_call(
        finish_kernel,
        out_shape=jax.ShapeDtypeStruct(matrix.shape, jnp.float32),
        in_specs=[VMEM] * 4,
        out_specs=VMEM,
        name="finish",
    )(panel, gain, y_part, matrix)


def to_all(value, axis, groups):
    count = len(groups[0])
    return lax.all_to_all(jnp.broadcast_to(value[None], (count,) + value.shape), axis, 0, 0, axis_index_groups=groups)


def per_device(covariance):
    tile_rows, nb, tile_cols, _ = covariance.shape
    col_count = lax.axis_size("col")
    my_col = lax.axis_index("col")
    matrix = covariance.reshape(tile_rows, nb * tile_cols, nb)
    along_z = [[z * NX + x for z in range(NZ)] for x in range(NX)]
    along_x = [[z * NX + x for x in range(NX)] for z in range(NZ)]
    along_y = [[c for c in range(q, col_count, 2)] for q in range(2)]
    pairs = [[c, c + 1] for c in range(0, col_count, 2)]
    half, quarter = col_count // 2, col_count // 4

    mine = covariance[:, :, 0, :].reshape(tile_rows * nb, nb)
    far = lax.ppermute(mine, "col", [(c, c + half) for c in range(PANELS)])
    mine = jnp.where(my_col >= half, far, mine)
    mid = lax.ppermute(mine, "col", [(c + h, c + h + quarter) for c in range(PANELS) for h in (0, half)])
    mine = jnp.where(my_col % half >= quarter, mid, mine)
    steps = []
    for start in range(0, col_count, quarter):
        steps += [(start, start + 2), (start + 1, start + 3), (start + 2, start)]
    near = lax.ppermute(mine, "col", steps)
    piece = lax.all_to_all(matrix[0].reshape(NZ, PART * tile_cols, nb), "row", 0, 0, axis_index_groups=along_z)[0]
    head = piece.reshape(PART, tile_cols, nb)[:, 0, :]
    own = to_all(head, "col", along_y)[:2]
    got = to_all(jnp.concatenate([own.reshape(2 * PART, nb), piece], axis=0), "row", along_x)
    first_core = my_col % 2 == 0
    lead = [
        got[0, :PART],
        jnp.where(first_core, got[0, PART : 2 * PART], got[1, :PART]),
        jnp.where(first_core, got[2, PART : 2 * PART], got[2, :PART]),
    ]
    lead = jnp.concatenate(lead, axis=0)
    lead = to_all(lead, "row", along_z)
    sent = jnp.concatenate([lead.reshape(NZ * PANELS * PART, nb), mine, near], axis=0)
    gathered = lax.all_gather(sent, "col", axis_index_groups=pairs)
    cols = pack(pack_cols_kernel, got, PANELS * PART * tile_cols)
    y_part = lax.all_to_all(cols, "row", 0, 0, axis_index_groups=along_z)
    panel, gain = factor(gathered)
    out = finish(panel, gain, y_part, matrix)
    return out.reshape(covariance.shape)


def solution(mesh):
    placed = (P(None, "row", None, "col"),)
    return jax.shard_map(
        per_device,
        mesh=mesh,
        in_specs=placed,
        out_specs=P(None, "row", None, "col"),
        check_vma=False,
    )
```
